32 devices in a mesh: pipe: 2 (over x), expert: 16 (over z, y, core).
Axes of the slice: x: 2, y: 2, z: 4, core: 2. Of those that a mesh axis runs over, the one named last changes fastest.
Arguments:
- tokens: bfloat16 [2048, 1024], P('expert'), may hold values from -6 to 6
- out_grad: bfloat16 [2048, 1024], P('expert'), may hold values from -6 to 6
- routes: int32 [2048, 6], P('expert'), may hold values from 0 to 15, as said below
- slots: int32 [2048, 6], P('expert'), may hold values from 0 to 63, as said below
- gates: bfloat16 [2048, 6], P('expert'), may hold values from 0.099609375 to 1
- w_gate: bfloat16 [16, 1408, 1024], P('expert', 'pipe'), may hold values from -0.1875 to 0.1875
- w_up: bfloat16 [16, 1408, 1024], P('expert', 'pipe'), may hold values from -0.1875 to 0.1875
- w_down: bfloat16 [16, 1408, 1024], P('expert', 'pipe'), may hold values from -0.15625 to 0.15625
Outputs:
- mixed: bfloat16 [2048, 1024], P('expert', 'pipe')
- grad_tokens: bfloat16 [2048, 1024], P('expert', 'pipe')
- grad_gates: float32 [2048, 6], P('expert')
- grad_w_gate: bfloat16 [16, 1408, 1024], P('expert', 'pipe')
- grad_w_up: bfloat16 [16, 1408, 1024], P('expert', 'pipe')
- grad_w_down: bfloat16 [16, 1408, 1024], P('expert', 'pipe')
The draws below stay inside these ranges and needn't reach their ends.
Inputs may be any that keep to these rules, and one draw needn't show every extreme that they name: `routes`: each token names 6 different experts. Within one device's block of 128 tokens no expert is named more than 64 times, and some expert is named exactly 64 times by every block. Within one block of 128 tokens the pairs (routes, slots) are all different.
All inputs are finite; a program needn't handle non-finite values.
Results may differ from the reference program's by a relative error of at most 0.015.
Values may be sent and summed in bfloat16 or wider, within the bound.
A program may use at most 64 MiB of HBM per device.

```python
import math
import jax
import jax.numpy as jnp
from jax import lax

D = 1024
FF = 1408
TOPK = 6
TOK_DEV = 128
EXPERTS = 16
TOKENS = 2048
EXPERT_ROW_LIMIT = 64
N_PIPE = 2


def assign_all(key):
    blocks = TOKENS // TOK_DEV
    total = TOK_DEV * TOPK
    others = EXPERTS - 1
    base_rows = (total - EXPERT_ROW_LIMIT) // others
    leftover_rows = total - EXPERT_ROW_LIMIT - base_rows * others
    pair_count = others // 2
    hottest = jax.random.randint(jax.random.fold_in(key, 11), (), 0, EXPERTS)

    def one_block(block_key):
        key_order, key_delta, key_slot, key_token = jax.random.split(block_key, 4)
        order = jax.random.permutation(key_order, EXPERTS).astype(jnp.int32)
        places = jnp.arange(EXPERTS, dtype=jnp.int32)
        hot_expert_flag = order == hottest
        hot_place = jnp.sum(jnp.where(hot_expert_flag, places, 0))
        cold_expert_index = places - (places > hot_place).astype(jnp.int32)
        extra_rows = (cold_expert_index < leftover_rows).astype(jnp.int32)
        delta = jax.random.randint(key_delta, (max(pair_count, 1),), 0, base_rows // 4 + 1)
        pair_index = jnp.minimum(cold_expert_index // 2, max(pair_count, 1) - 1)
        in_pair = cold_expert_index < 2 * pair_count
        signed = jnp.where(cold_expert_index % 2 == 0, 1, -1)
        shift_amount = jnp.where(in_pair, signed * delta[pair_index], 0)
        expert_loads = jnp.where(hot_expert_flag, EXPERT_ROW_LIMIT, base_rows + extra_rows + shift_amount).astype(jnp.int32)
        ends = jnp.cumsum(expert_loads)
        starts = ends - expert_loads
        spots = jnp.arange(total, dtype=jnp.int32)
        which = jnp.sum((spots[:, None] >= ends[None, :]).astype(jnp.int32), axis=1)
        label = order[which]
        rank = spots - starts[which]
        slot_perm = jax.vmap(lambda sub: jax.random.permutation(sub, EXPERT_ROW_LIMIT))(jax.random.split(key_slot, EXPERTS)).astype(jnp.int32)
        slot_val = slot_perm[label, rank]
        label_grid = label.reshape(TOPK, TOK_DEV).T
        slot_grid = slot_val.reshape(TOPK, TOK_DEV).T
        shuffle = jax.random.permutation(key_token, TOK_DEV)
        return (label_grid[shuffle], slot_grid[shuffle])
    keys = jax.random.split(jax.random.fold_in(key, 7), blocks)
    label_all, slot_all = jax.vmap(one_block)(keys)
    return (label_all.reshape(TOKENS, TOPK).astype(jnp.int32), slot_all.reshape(TOKENS, TOPK).astype(jnp.int32))


def draw_routes(key, part):
    return assign_all(key)[0]


def draw_slots(key, part):
    return assign_all(key)[1]


def block_levels(rng, dims, cuts, least, high):
    def one(axis_at, blocks):
        steps = jax.random.uniform(jax.random.fold_in(jax.random.fold_in(rng, 6), axis_at), (blocks,), jnp.float32, least / len(cuts), high / len(cuts))
        return jnp.repeat(jnp.exp(steps), dims[axis_at] // blocks).reshape((-1,) + (1,) * (len(dims) - axis_at - 1))

    loudness = one(*cuts[0])
    for cut in cuts[1:]:
        loudness = loudness * one(*cut)
    return loudness


def noise(key, dims, spread, limit, cuts=(), held_as=jnp.bfloat16):
    loudness = block_levels(key, dims, cuts, -0.22, 0.18) if cuts else 1.0
    values = jax.random.normal(key, dims, jnp.float32) * spread * loudness
    return jnp.minimum(jnp.maximum(values, -limit), limit).astype(held_as)


def setup_inputs(seed: int = 0) -> dict:
    seeds = jax.random.split(jax.random.key(seed), 9)
    return {
        "tokens": noise(seeds[0], (TOKENS, D), 1.0, 6.0, ((0, 16),)),
        "out_grad": noise(seeds[1], (TOKENS, D), 1.0, 6.0, ((0, 16),)),
        "routes": draw_routes(jax.random.fold_in(seeds[8], 71), 0),
        "slots": draw_slots(jax.random.fold_in(seeds[8], 71), 0),
        "gates": jnp.clip(jnp.exp(math.log(1.0) - 2.306499 * jax.random.uniform(seeds[4], (TOKENS, TOPK), jnp.float32) ** block_levels(seeds[4], (TOKENS, TOPK), ((0, 16),), -0.2, 0.2)), 0.099609375, 1.0).astype(jnp.bfloat16),
        "w_gate": noise(seeds[5], (EXPERTS, FF, D), D ** -0.5, 0.1875, ((0, 16), (1, 2))),
        "w_up": noise(seeds[6], (EXPERTS, FF, D), D ** -0.5, 0.1875, ((0, 16), (1, 2))),
        "w_down": noise(seeds[7], (EXPERTS, FF, D), FF ** -0.5, 0.15625, ((0, 16), (1, 2))),
    }


def reference(tokens, out_grad, routes, slots, gates, w_gate, w_up, w_down):
    blocks = TOKENS // TOK_DEV
    buffer_rows = blocks * EXPERT_ROW_LIMIT
    hidden_block = FF // N_PIPE
    assign_count = TOKENS * TOPK
    assign_ids = jnp.arange(assign_count, dtype=jnp.int32)
    token_ids = assign_ids // TOPK
    source = token_ids // TOK_DEV
    flat_routes = routes.reshape(-1).astype(jnp.int32)
    flat_slots = slots.reshape(-1).astype(jnp.int32)
    position = (flat_routes * blocks + source) * EXPERT_ROW_LIMIT + flat_slots
    table = jnp.full((EXPERTS * buffer_rows,), assign_count, jnp.int32).at[position].set(assign_ids)
    table = table.reshape(EXPERTS, buffer_rows)
    flat_gates = gates.reshape(-1)
    contract = (((1,), (1,)), ((), ()))
    over_rows = (((0,), (0,)), ((), ()))

    def per_expert(carry, inputs):
        mixed_acc, grad_acc, gate_acc = carry
        assigned, gate_w, up_w, down_w = inputs
        row_token = jnp.where(assigned < assign_count, assigned // TOPK, TOKENS).astype(jnp.int32)
        x_rows = jnp.take(tokens, row_token, axis=0, mode="fill", fill_value=0)
        y_rows = jnp.take(out_grad, row_token, axis=0, mode="fill", fill_value=0)
        g_rows = jnp.take(flat_gates, assigned, axis=0, mode="fill", fill_value=0)
        gate_pre = lax.dot_general(x_rows, gate_w, contract, preferred_element_type=jnp.float32)
        up_pre = lax.dot_general(x_rows, up_w, contract, preferred_element_type=jnp.float32)
        sigma = jax.nn.sigmoid(gate_pre)
        silu_val = gate_pre * sigma
        act = (silu_val * up_pre).astype(jnp.bfloat16)
        act3 = act.astype(jnp.float32).reshape(buffer_rows, N_PIPE, hidden_block)
        down3 = down_w.astype(jnp.float32).reshape(N_PIPE, hidden_block, D)
        parts = jnp.einsum("rjh,jhd->jrd", act3, down3).astype(jnp.bfloat16)
        out_sum = jnp.sum(parts.astype(jnp.float32), axis=0)
        d_out = (g_rows.astype(jnp.float32)[:, None] * y_rows.astype(jnp.float32)).astype(jnp.bfloat16)
        d_act = lax.dot_general(d_out, down_w, contract, preferred_element_type=jnp.float32)
        d_gate = (d_act * up_pre * sigma * (1.0 + gate_pre * (1.0 - sigma))).astype(jnp.bfloat16)
        d_up = (d_act * silu_val).astype(jnp.bfloat16)
        gate3 = gate_w.astype(jnp.float32).reshape(N_PIPE, hidden_block, D)
        up3 = up_w.astype(jnp.float32).reshape(N_PIPE, hidden_block, D)
        dg3 = d_gate.astype(jnp.float32).reshape(buffer_rows, N_PIPE, hidden_block)
        du3 = d_up.astype(jnp.float32).reshape(buffer_rows, N_PIPE, hidden_block)
        back_parts = (jnp.einsum("rjh,jhd->jrd", dg3, gate3) + jnp.einsum("rjh,jhd->jrd", du3, up3)).astype(jnp.bfloat16)
        back_sum = jnp.sum(back_parts.astype(jnp.float32), axis=0)
        mixed_acc = mixed_acc.at[row_token].add(g_rows.astype(jnp.float32)[:, None] * out_sum, mode="drop")
        grad_acc = grad_acc.at[row_token].add(back_sum, mode="drop")
        gate_val = jnp.sum(y_rows.astype(jnp.float32) * out_sum, axis=1)
        gate_acc = gate_acc.at[assigned].set(gate_val, mode="drop")
        grad_gate_w = lax.dot_general(d_gate, x_rows, over_rows, preferred_element_type=jnp.float32).astype(jnp.bfloat16)
        grad_up_w = lax.dot_general(d_up, x_rows, over_rows, preferred_element_type=jnp.float32).astype(jnp.bfloat16)
        grad_down_w = lax.dot_general(act, d_out, over_rows, preferred_element_type=jnp.float32).astype(jnp.bfloat16)
        return (mixed_acc, grad_acc, gate_acc), (grad_gate_w, grad_up_w, grad_down_w)

    start = (jnp.zeros((TOKENS, D), jnp.float32), jnp.zeros((TOKENS, D), jnp.float32), jnp.zeros((assign_count,), jnp.float32))
    final, grads = lax.scan(per_expert, start, (table, w_gate, w_up, w_down))
    mixed_acc, grad_acc, gate_acc = final
    return (mixed_acc.astype(jnp.bfloat16), grad_acc.astype(jnp.bfloat16), gate_acc.reshape(TOKENS, TOPK), grads[0], grads[1], grads[2])
```

```python
import functools

import jax
import jax.numpy as jnp
from jax import lax
from jax.experimental import pallas as pl
from jax.experimental.pallas import tpu as pltpu
from jax.sharding import PartitionSpec as P

INNER = 2
BF16 = jnp.bfloat16
F32 = jnp.float32


def place(experts):
    me = lax.axis_index("expert")
    return me, me // (INNER * INNER), (me // INNER) % INNER, me % INNER


def join(outer, mid, low):
    return (outer * INNER + mid) * INNER + low


def peer(expert=None, pipe=None):
    p = lax.axis_index("pipe") if pipe is None else pipe
    e = lax.axis_index("expert") if expert is None else expert
    return (p, e)


def meet(pipes, experts):
    p = lax.axis_index("pipe")
    e = lax.axis_index("expert")
    barrier = pltpu.get_barrier_semaphore()
    for d in range(1, experts):
        pl.semaphore_signal(barrier, inc=1, device_id=peer(expert=(e + d) % experts),
                            device_id_type=pl.DeviceIdType.MESH)
    for d in range(1, pipes):
        pl.semaphore_signal(barrier, inc=1, device_id=peer(pipe=(p + d) % pipes),
                            device_id_type=pl.DeviceIdType.MESH)
    pl.semaphore_wait(barrier, experts + pipes - 2)


def remote(src, dst, send, recv, dev):
    return pltpu.make_async_remote_copy(src_ref=src, dst_ref=dst, send_sem=send, recv_sem=recv,
                                        device_id=dev, device_id_type=pl.DeviceIdType.MESH)


def gather_plan(pipes, experts):
    outer = experts // (INNER * INNER)
    lanes = 2 * outer - 1
    base = {"z": 0, "y": outer - 1, "own": 2 * outer - 1, "c": 2 * outer, "x": 2 * outer + lanes}
    base["cx"] = base["x"] + lanes
    return outer, lanes, base, base["cx"] + lanes


def gather_kernel(pipes, experts, x, dy, meta, xg, dyg, mg, send, recv, msend, mrecv, local):
    me, z, y, c = place(experts)
    p = lax.axis_index("pipe")
    outer, lanes, base, count = gather_plan(pipes, experts)
    width = x.shape[1]
    side = (width // 128 * 3 // 8) * 128
    par = p % 2
    wide = pl.ds(pl.multiple_of(par * side, 128), width - side)
    give = pl.ds(pl.multiple_of(par * (width - side), 128), side)
    take = pl.ds(pl.multiple_of((1 - par) * (width - side), 128), side)
    xpeer = peer(pipe=p + 1 - 2 * par)
    cpeer = peer(expert=join(z, y, 1 - c))
    ypeer = peer(expert=join(z, 1 - y, c))
    own = [pltpu.make_async_copy(s, g.at[me], local.at[i])
           for i, (s, g) in enumerate(((x, xg), (dy, dyg), (meta, mg)))]
    for copy in own:
        copy.start()
    meet(pipes, experts)
    sent = []

    def go(src, dst, s, r, dev):
        copy = remote(src, dst, s, r, dev)
        copy.start()
        sent.append(copy)

    for d in range(1, experts):
        go(meta, mg.at[me], msend.at[d - 1], mrecv.at[d - 1], peer(expert=(me + d) % experts))
    arrays = ((x, xg), (dy, dyg))

    def sems(a, i):
        return send.at[a * count + i], recv.at[a * count + i]

    def arrived(ref, a, i):
        remote(ref, ref, *sems(a, i), cpeer).wait_recv()

    for a, (s, g) in enumerate(arrays):
        for d in range(1, outer):
            go(s.at[:, wide], g.at[me, :, wide], *sems(a, base["z"] + d - 1),
               peer(expert=join((z + d) % outer, y, c)))
        go(s.at[:, wide], g.at[me, :, wide], *sems(a, base["y"]), ypeer)
        go(s, g.at[me], *sems(a, base["own"]), cpeer)
    for a, (s, g) in enumerate(arrays):
        for d in range(1, outer):
            b = join((z + outer - d) % outer, y, c)
            arrived(g.at[b, :, wide], a, base["z"] + d - 1)
            go(g.at[b, :, wide], g.at[b, :, wide], *sems(a, base["y"] + d), ypeer)
            go(g.at[b, :, give], g.at[b, :, give], *sems(a, base["x"] + d - 1), xpeer)
            go(g.at[b, :, wide], g.at[b, :, wide], *sems(a, base["c"] + d - 1), cpeer)
        for d in range(outer):
            b = join((z + outer - d) % outer, 1 - y, c)
            arrived(g.at[b, :, wide], a, base["y"] + d)
            go(g.at[b, :, give], g.at[b, :, give], *sems(a, base["x"] + outer - 1 + d), xpeer)
            go(g.at[b, :, wide], g.at[b, :, wide], *sems(a, base["c"] + outer - 1 + d), cpeer)
    for a, (s, g) in enumerate(arrays):
        for i in range(lanes):
            b = (join((z + outer - i - 1) % outer, y, c) if i < outer - 1
                 else join((z + outer - (i - outer + 1)) % outer, 1 - y, c))
            arrived(g.at[b, :, take], a, base["x"] + i)
            go(g.at[b, :, take], g.at[b, :, take], *sems(a, base["cx"] + i), cpeer)
    for a, (s, g) in enumerate(arrays):
        arrived(g.at[join(z, y, 1 - c)], a, base["own"])
        for i in range(lanes):
            b = (join((z + outer - i - 1) % outer, y, 1 - c) if i < outer - 1
                 else join((z + outer - (i - outer + 1)) % outer, 1 - y, 1 - c))
            arrived(g.at[b, :, wide], a, base["c"] + i)
            arrived(g.at[b, :, take], a, base["cx"] + i)
    for d in range(1, experts):
        b = (me + experts - d) % experts
        remote(mg.at[b], mg.at[b], msend.at[d - 1], mrecv.at[d - 1], cpeer).wait_recv()
    for copy in sent:
        copy.wait_send()
    for copy in own:
        copy.wait()


def gather_all(pipes, experts, x, dy, meta):
    count = gather_plan(pipes, experts)[3]
    hbm = pl.BlockSpec(memory_space=pl.ANY)
    vmem = pl.BlockSpec(memory_space=pltpu.VMEM)
    return pl.pallas_call(
        functools.partial(gather_kernel, pipes, experts),
        out_shape=[jax.ShapeDtypeStruct((experts,) + v.shape, v.dtype) for v in (x, dy, meta)],
        in_specs=[vmem] * 3,
        out_specs=[hbm] * 3,
        scratch_shapes=[
            pltpu.SemaphoreType.DMA((2 * count,)),
            pltpu.SemaphoreType.DMA((2 * count,)),
            pltpu.SemaphoreType.DMA((experts - 1,)),
            pltpu.SemaphoreType.DMA((experts - 1,)),
            pltpu.SemaphoreType.DMA((3,)),
        ],
        compiler_params=pltpu.CompilerParams(collective_id=0, has_side_effects=True),
        name="gather_rows",
    )(x, dy, meta)


def reduce_plan(pipes, experts):
    outer = experts // (INNER * INNER)
    groups = min(outer, 4)
    chunks = 2 * groups
    base = {"c": 0, "x": chunks, "y": chunks * pipes}
    base["z"] = base["y"] + groups
    return outer, groups, base, base["z"] + outer - 1


def reduce_kernel(pipes, experts, pm, pg, gate, om, og, ogate,
                  stay, come, xin, half, yin, line, zin, gin, gx,
                  send, recv, gsend, grecv, gxs, gxr, local):
    me, z, y, c = place(experts)
    p = lax.axis_index("pipe")
    outer, groups, base, count = reduce_plan(pipes, experts)
    size = outer // groups
    chunks = 2 * groups
    share = om.shape[1]
    cpeer = peer(expert=join(z, y, 1 - c))
    ypeer = peer(expert=join(z, 1 - y, c))
    mine = pl.ds(pl.multiple_of(p * share, 128), share)
    parts = (pm, pg)
    outs = (om, og)

    def where(k):
        g = (z // size + 1 + k % groups) % groups
        return (y + 1 + k // groups) % 2, pl.ds(g * size, size)

    def where_peer(k):
        return where(k)

    loads = []
    for a in range(2):
        for k in range(chunks):
            yy, zz = where(k)
            copy = pltpu.make_async_copy(parts[a].at[zz, yy, c], stay.at[a, yy, zz],
                                         local.at[a * chunks + k])
            copy.start()
            loads.append(copy)
    keep = pltpu.make_async_copy(gate.at[me], gin.at[me], local.at[2 * chunks])
    keep.start()
    meet(pipes, experts)
    sent = []

    def sems(a, i):
        return send.at[a * count + i], recv.at[a * count + i]

    def go(src, dst, s, r, dev):
        copy = remote(src, dst, s, r, dev)
        copy.start()
        sent.append(copy)

    def arrived(ref, a, i):
        remote(ref, ref, *sems(a, i), cpeer).wait_recv()

    for d in range(1, experts):
        to = (me + d) % experts
        go(gate.at[to], gin.at[me], gsend.at[d - 1], grecv.at[d - 1], peer(expert=to))
    for a in range(2):
        for k in range(chunks):
            yy, zz = where(k)
            go(parts[a].at[zz, yy, 1 - c], come.at[a, yy, zz], *sems(a, base["c"] + k), cpeer)

    def core_step(a, k):
        yy, zz = where(k)
        loads[a * chunks + k].wait()
        arrived(come.at[a, yy, zz], a, base["c"] + k)
        stay[a, yy, zz] = (stay[a, yy, zz].astype(F32) + come[a, yy, zz].astype(F32)).astype(BF16)
        for j in range(1, pipes):
            to = (p + j) % pipes
            cols = pl.ds(pl.multiple_of(to * share, 128), share)
            go(stay.at[a, yy, zz, :, cols], xin.at[a, j - 1, yy, zz],
               *sems(a, base["x"] + (j - 1) * chunks + k), peer(pipe=to))

    def x_step(a, k):
        yy, zz = where(k)
        total = stay[a, yy, zz, :, mine].astype(F32)
        for j in range(1, pipes):
            arrived(xin.at[a, j - 1, yy, zz], a, base["x"] + (j - 1) * chunks + k)
            total = total + xin[a, j - 1, yy, zz].astype(F32)
        half[a, yy, zz] = total.astype(BF16)
        if k < groups:
            go(half.at[a, yy, zz], yin.at[a, zz], *sems(a, base["y"] + k), ypeer)

    def y_step(a, k):
        yy, zz = where(groups + k)
        arrived(yin.at[a, zz], a, base["y"] + k)
        line[a, zz] = (half[a, yy, zz].astype(F32) + yin[a, zz].astype(F32)).astype(BF16)
        if size == 1 and k < groups - 1:
            z_send(a, k + 1)

    def z_send(a, d):
        to = (z + d) % outer
        go(line.at[a, to], zin.at[a, d - 1], *sems(a, base["z"] + d - 1),
           peer(expert=join(to, y, c)))

    for a in range(2):
        for k in range(chunks):
            core_step(a, k)
    for d in range(1, experts):
        b = (me + experts - d) % experts
        remote(gin.at[b], gin.at[b], gsend.at[d - 1], grecv.at[d - 1], cpeer).wait_recv()
    keep.wait()
    for j in range(1, pipes):
        go(gin, gx.at[j - 1], gxs.at[j - 1], gxr.at[j - 1], peer(pipe=(p + j) % pipes))
    for a in range(2):
        for k in range(chunks):
            x_step(a, k)
        for k in range(groups):
            y_step(a, k)
        if size > 1:
            for d in range(1, outer):
                z_send(a, d)
    whole = gin[...]
    for j in range(1, pipes):
        remote(gin, gx.at[j - 1], gxs.at[j - 1], gxr.at[j - 1], cpeer).wait_recv()
        whole = whole + gx[j - 1]
    ogate[...] = whole
    for a in range(2):
        total = line[a, z].astype(F32)
        for d in range(1, outer):
            arrived(zin.at[a, d - 1], a, base["z"] + d - 1)
            total = total + zin[a, d - 1].astype(F32)
        outs[a][...] = total.astype(BF16)
    for copy in sent:
        copy.wait_send()


def reduce_all(pipes, experts, mixed, grad, gate):
    outer, groups, base, count = reduce_plan(pipes, experts)
    rows, width = mixed.shape[1:]
    share = width // pipes
    shape = (outer, INNER, INNER, rows, width)
    hbm = pl.BlockSpec(memory_space=pl.ANY)
    vmem = pl.BlockSpec(memory_space=pltpu.VMEM)
    return pl.pallas_call(
        functools.partial(reduce_kernel, pipes, experts),
        out_shape=[jax.ShapeDtypeStruct((rows, share), BF16)] * 2
        + [jax.ShapeDtypeStruct(gate.shape, F32)],
        in_specs=[hbm, hbm, vmem],
        out_specs=[vmem] * 3,
        scratch_shapes=[
            pltpu.VMEM((2, INNER, outer, rows, width), BF16),
            pltpu.VMEM((2, INNER, outer, rows, width), BF16),
            pltpu.VMEM((2, pipes - 1, INNER, outer, rows, share), BF16),
            pltpu.VMEM((2, INNER, outer, rows, share), BF16),
            pltpu.VMEM((2, outer, rows, share), BF16),
            pltpu.VMEM((2, outer, rows, share), BF16),
            pltpu.VMEM((2, outer - 1, rows, share), BF16),
            pltpu.VMEM(gate.shape, F32),
            pltpu.VMEM((pipes - 1,) + gate.shape, F32),
            pltpu.SemaphoreType.DMA((2 * count,)),
            pltpu.SemaphoreType.DMA((2 * count,)),
            pltpu.SemaphoreType.DMA((experts - 1,)),
            pltpu.SemaphoreType.DMA((experts - 1,)),
            pltpu.SemaphoreType.DMA((pipes - 1,)),
            pltpu.SemaphoreType.DMA((pipes - 1,)),
            pltpu.SemaphoreType.DMA((4 * groups + 1,)),
        ],
        compiler_params=pltpu.CompilerParams(collective_id=1, has_side_effects=True),
        name="reduce_rows",
    )(mixed.reshape(shape), grad.reshape(shape), gate)


def body(tokens, out_grad, routes, slots, gates, w_gate, w_up, w_down):
    local_tokens, topk = routes.shape
    pipes = lax.axis_size("pipe")
    experts = lax.axis_size("expert")
    capacity = 4 * local_tokens * topk // (3 * experts)
    width = tokens.shape[1]
    half = (topk + 7) // 8 * 8
    position = (routes * capacity + slots).astype(F32)
    pad = jnp.zeros((local_tokens, half - topk), F32)
    meta = jnp.concatenate([position, pad, gates.astype(F32), pad], axis=1).T
    xg, dyg, mg = gather_all(pipes, experts, tokens, out_grad, meta)

    rows = experts * capacity
    first = lax.axis_index("expert") * capacity
    wanted = (first + jnp.arange(capacity)).astype(F32)
    hit = mg[:, :topk, None, :] == wanted[None, None, :, None]
    pick = jnp.sum(hit.astype(F32), axis=1).astype(BF16)
    weigh = jnp.sum(jnp.where(hit, mg[:, half:half + topk, None, :], 0.0), axis=1).astype(BF16)
    by_token = (((2,), (1,)), ((0,), (0,)))

    def select(matrix, source):
        picked = lax.dot_general(matrix, source, by_token, preferred_element_type=F32)
        return picked.astype(BF16).reshape(rows, width)

    x = select(pick, xg)
    dy = select(pick, dyg)
    d_out = select(weigh, dyg)
    gate_w, up_w, down_w = w_gate[0], w_up[0], w_down[0]
    contract = (((1,), (1,)), ((), ()))
    over_rows = (((0,), (0,)), ((), ()))
    dot = functools.partial(lax.dot_general, preferred_element_type=F32)
    plain = (((1,), (0,)), ((), ()))
    gate_pre = dot(x, gate_w, contract)
    up_pre = dot(x, up_w, contract)
    sigma = jax.nn.sigmoid(gate_pre)
    silu_val = gate_pre * sigma
    act = (silu_val * up_pre).astype(BF16)
    partial_out = dot(act, down_w, plain).astype(BF16)
    d_act = dot(d_out, down_w, contract)
    d_gate = (d_act * up_pre * sigma * (1.0 + gate_pre * (1.0 - sigma))).astype(BF16)
    d_up = (d_act * silu_val).astype(BF16)
    partial_back = (dot(d_gate, gate_w, plain) + dot(d_up, up_w, plain)).astype(BF16)
    grad_gate_w = dot(d_gate, x, over_rows).astype(BF16)
    grad_up_w = dot(d_up, x, over_rows).astype(BF16)
    grad_down_w = dot(act, d_out, over_rows).astype(BF16)

    over_slots = (((1,), (1,)), ((0,), (0,)))
    shape = (experts, capacity, width)
    mixed_part = dot(weigh, partial_out.reshape(shape), over_slots).astype(BF16)
    grad_part = dot(pick, partial_back.reshape(shape), over_slots).astype(BF16)
    row_gate = jnp.sum(dy.astype(F32) * partial_out.astype(F32), axis=1).reshape(experts, capacity)
    gate_part = jnp.sum(pick.astype(F32) * row_gate[:, :, None], axis=1)
    gate_part = jnp.broadcast_to(gate_part[:, None, :], (experts, 8, local_tokens))
    mixed, grad_total, gate_all = reduce_all(pipes, experts, mixed_part, grad_part, gate_part)
    named = routes[:, :, None] == jnp.arange(experts)[None, None, :]
    grad_gates = jnp.sum(jnp.where(named, gate_all[:, 0, :].T[:, None, :], 0.0), axis=2)
    return (mixed, grad_total, grad_gates, grad_gate_w[None], grad_up_w[None], grad_down_w[None])


def solution(mesh):
    rows = P("expert", None)
    weights = P("expert", "pipe", None)
    return jax.shard_map(
        body,
        mesh=mesh,
        in_specs=(rows,) * 5 + (weights,) * 3,
        out_specs=(P("expert", "pipe"), P("expert", "pipe"), rows) + (weights,) * 3,
        check_vma=False,
    )
```

```python
import functools

import jax
import jax.numpy as jnp
from jax import lax
from jax.experimental import pallas as pl
from jax.experimental.pallas import tpu as pltpu
from jax.sharding import PartitionSpec as P

INNER = 2
BF16 = jnp.bfloat16
F32 = jnp.float32


def place(experts):
    me = lax.axis_index("expert")
    return me, me // (INNER * INNER), (me // INNER) % INNER, me % INNER


def join(outer, mid, low):
    return (outer * INNER + mid) * INNER + low


def peer(expert=None, pipe=None):
    p = lax.axis_index("pipe") if pipe is None else pipe
    e = lax.axis_index("expert") if expert is None else expert
    return (p, e)


def meet(pipes, experts):
    p = lax.axis_index("pipe")
    e = lax.axis_index("expert")
    barrier = pltpu.get_barrier_semaphore()
    for d in range(1, experts):
        pl.semaphore_signal(barrier, inc=1, device_id=peer(expert=(e + d) % experts),
                            device_id_type=pl.DeviceIdType.MESH)
    for d in range(1, pipes):
        pl.semaphore_signal(barrier, inc=1, device_id=peer(pipe=(p + d) % pipes),
                            device_id_type=pl.DeviceIdType.MESH)
    pl.semaphore_wait(barrier, experts + pipes - 2)


def remote(src, dst, send, recv, dev):
    return pltpu.make_async_remote_copy(src_ref=src, dst_ref=dst, send_sem=send, recv_sem=recv,
                                        device_id=dev, device_id_type=pl.DeviceIdType.MESH)


def gather_plan(pipes, experts):
    outer = experts // (INNER * INNER)
    lanes = 2 * outer - 1
    base = {"z": 0, "y": outer - 1, "own": 2 * outer - 1, "c": 2 * outer, "x": 2 * outer + lanes}
    base["cx"] = base["x"] + lanes
    base["down"] = base["cx"] + lanes
    return outer, lanes, base, base["down"] + outer - 1


def gather_kernel(pipes, experts, x, dy, meta, xg, dyg, mg, send, recv, msend, mrecv, local):
    me, z, y, c = place(experts)
    p = lax.axis_index("pipe")
    outer, lanes, base, count = gather_plan(pipes, experts)
    width = x.shape[1]
    side = (width // 128 * 3 // 8) * 128
    par = p % 2
    wide = pl.ds(pl.multiple_of(par * side, 128), width - side)
    give = pl.ds(pl.multiple_of(par * (width - side), 128), side)
    take = pl.ds(pl.multiple_of((1 - par) * (width - side), 128), side)
    xpeer = peer(pipe=p + 1 - 2 * par)
    cpeer = peer(expert=join(z, y, 1 - c))
    ypeer = peer(expert=join(z, 1 - y, c))
    own = [pltpu.make_async_copy(s, g.at[me], local.at[i])
           for i, (s, g) in enumerate(((x, xg), (dy, dyg), (meta, mg)))]
    for copy in own:
        copy.start()
    meet(pipes, experts)
    sent = []

    def go(src, dst, s, r, dev):
        copy = remote(src, dst, s, r, dev)
        copy.start()
        sent.append(copy)

    for d in range(1, experts):
        go(meta, mg.at[me], msend.at[d - 1], mrecv.at[d - 1], peer(expert=(me + d) % experts))
    arrays = ((x, xg), (dy, dyg))
    inner = jnp.minimum(z, outer - 1 - z)
    below_more = z > outer - 1 - z

    def nearest(n):
        paired = n < 2 * inner
        below = jnp.where(paired, n % 2 == 0, below_more)
        far = jnp.where(paired, n // 2 + 1, n - inner + 1)
        return below, jnp.where(below, far, outer - far)

    def sems(a, i):
        return send.at[a * count + i], recv.at[a * count + i]

    def arrived(ref, a, i):
        remote(ref, ref, *sems(a, i), cpeer).wait_recv()

    later = []

    def chain(src, block, a, up, down, slot_up, slot_down, dev_up, dev_down):
        g = arrays[a][1]
        for way, go_there, slot, dev in (("z", up, slot_up, dev_up),
                                         ("down", down, slot_down, dev_down)):
            copy = remote(src, g.at[block, :, wide], send.at[a * count + base[way] + slot - 1],
                          recv.at[a * count + base["z"] + slot - 1], dev)
            pl.when(go_there)(copy.start)
            later.append((go_there, copy))

    above = peer(expert=join(jnp.minimum(z + 1, outer - 1), y, c))
    under = peer(expert=join(jnp.maximum(z - 1, 0), y, c))

    def start(a):
        s, g = arrays[a]
        chain(s.at[:, wide], me, a, z < outer - 1, z > 0, 1, outer - 1, above, under)
        go(s.at[:, wide], g.at[me, :, wide], *sems(a, base["y"]), ypeer)
        go(s, g.at[me], *sems(a, base["own"]), cpeer)

    def z_event(a, n):
        g = arrays[a][1]
        below, d = nearest(n)
        b = join((z + outer - d) % outer, y, c)
        ref = g.at[b, :, wide]
        arrived(ref, a, base["z"] + d - 1)
        chain(ref, b, a, below & (z < outer - 1), jnp.logical_not(below) & (z > 0),
              jnp.minimum(d + 1, outer - 1), jnp.maximum(d - 1, 1), above, under)
        go(ref, ref, *sems(a, base["y"] + d), ypeer)
        go(g.at[b, :, give], g.at[b, :, give], *sems(a, base["x"] + d - 1), xpeer)
        go(ref, ref, *sems(a, base["c"] + d - 1), cpeer)

    def y_event(a, n):
        g = arrays[a][1]
        d = 0 if n < 0 else nearest(n)[1]
        b = join((z + outer - d) % outer, 1 - y, c)
        ref = g.at[b, :, wide]
        arrived(ref, a, base["y"] + d)
        go(g.at[b, :, give], g.at[b, :, give], *sems(a, base["x"] + outer - 1 + d), xpeer)
        go(ref, ref, *sems(a, base["c"] + outer - 1 + d), cpeer)

    def x_event(a, n, across):
        g = arrays[a][1]
        d = 0 if n < 0 else nearest(n)[1]
        b = join((z + outer - d) % outer, 1 - y if across else y, c)
        i = outer - 1 + d if across else d - 1
        arrived(g.at[b, :, take], a, base["x"] + i)
        go(g.at[b, :, take], g.at[b, :, take], *sems(a, base["cx"] + i), cpeer)

    steps = []
    for a in range(2):
        at = 2 * outer * a
        steps += [(at - 1, start, (a,))] if a else []
        steps += [(at + 2 * n, z_event, (a, n)) for n in range(outer - 1)]
        steps += [(at + 2 * n + 3, y_event, (a, n)) for n in range(-1, outer - 1)]
        steps += [(at + 2 * n + 6, x_event, (a, n, False)) for n in range(outer - 1)]
        steps += [(at + 2 * n + 8, x_event, (a, n, True)) for n in range(-1, outer - 1)]
    start(0)
    for _, run, args in sorted(steps, key=lambda step: step[0]):
        run(*args)
    for a, (s, g) in enumerate(arrays):
        arrived(g.at[join(z, y, 1 - c)], a, base["own"])
        for i in range(lanes):
            b = (join((z + outer - i - 1) % outer, y, 1 - c) if i < outer - 1
                 else join((z + outer - (i - outer + 1)) % outer, 1 - y, 1 - c))
            arrived(g.at[b, :, wide], a, base["c"] + i)
            arrived(g.at[b, :, take], a, base["cx"] + i)
    for go_there, copy in later:
        pl.when(go_there)(copy.wait_send)
    for d in range(1, experts):
        b = (me + experts - d) % experts
        remote(mg.at[b], mg.at[b], msend.at[d - 1], mrecv.at[d - 1], cpeer).wait_recv()
    for copy in sent:
        copy.wait_send()
    for copy in own:
        copy.wait()


def gather_all(pipes, experts, x, dy, meta):
    count = gather_plan(pipes, experts)[3]
    hbm = pl.BlockSpec(memory_space=pl.ANY)
    vmem = pl.BlockSpec(memory_space=pltpu.VMEM)
    return pl.pallas_call(
        functools.partial(gather_kernel, pipes, experts),
        out_shape=[jax.ShapeDtypeStruct((experts,) + v.shape, v.dtype) for v in (x, dy, meta)],
        in_specs=[vmem] * 3,
        out_specs=[hbm] * 3,
        scratch_shapes=[
            pltpu.SemaphoreType.DMA((2 * count,)),
            pltpu.SemaphoreType.DMA((2 * count,)),
            pltpu.SemaphoreType.DMA((experts - 1,)),
            pltpu.SemaphoreType.DMA((experts - 1,)),
            pltpu.SemaphoreType.DMA((3,)),
        ],
        compiler_params=pltpu.CompilerParams(collective_id=0, has_side_effects=True),
        name="gather_rows",
    )(x, dy, meta)


def reduce_plan(pipes, experts):
    outer = experts // (INNER * INNER)
    groups = min(outer, 4)
    chunks = 2 * groups
    sizes = (("c", chunks), ("xa", chunks * (pipes - 1)), ("ya", groups), ("yb", groups),
             ("xb", groups * (pipes - 1)), ("za", outer - 1), ("zb", outer - 1))
    base, total = {}, 0
    for name, size in sizes:
        base[name] = total
        total += size
    return outer, groups, base, total


def reduce_kernel(pipes, experts, pm, pg, gate, om, og, ogate,
                  stay, come, xain, half, yain, ybin, mid, xbin, line, zin, gin, gx,
                  send, recv, gsend, grecv, gxs, gxr, local):
    me, z, y, c = place(experts)
    p = lax.axis_index("pipe")
    outer, groups, base, count = reduce_plan(pipes, experts)
    size = outer // groups
    chunks = 2 * groups
    share = om.shape[1]
    top = om.shape[0] // 2
    rows_a, rows_b = pl.ds(0, top), pl.ds(top, top)
    cpeer = peer(expert=join(z, y, 1 - c))
    ypeer = peer(expert=join(z, 1 - y, c))
    mine = pl.ds(pl.multiple_of(p * share, 128), share)
    parts = (pm, pg)
    outs = (om, og)

    def where(k):
        g = (z // size + 1 + k % groups) % groups
        return (y + 1 + k // groups) % 2, pl.ds(g * size, size)

    loads = []
    for a in range(2):
        for k in range(chunks):
            yy, zz = where(k)
            copy = pltpu.make_async_copy(parts[a].at[zz, yy, c], stay.at[a, yy, zz],
                                         local.at[a * chunks + k])
            copy.start()
            loads.append(copy)
    keep = pltpu.make_async_copy(gate.at[me], gin.at[me], local.at[2 * chunks])
    keep.start()
    meet(pipes, experts)
    sent = []

    def sems(a, i):
        return send.at[a * count + i], recv.at[a * count + i]

    def go(src, dst, s, r, dev):
        copy = remote(src, dst, s, r, dev)
        copy.start()
        sent.append(copy)

    def arrived(ref, a, i):
        remote(ref, ref, *sems(a, i), cpeer).wait_recv()

    for d in range(1, experts):
        to = (me + d) % experts
        go(gate.at[to], gin.at[me], gsend.at[d - 1], grecv.at[d - 1], peer(expert=to))
    for a in range(2):
        for k in range(chunks):
            yy, zz = where(k)
            go(parts[a].at[zz, yy, 1 - c], come.at[a, yy, zz], *sems(a, base["c"] + k), cpeer)

    def plus(left, right):
        return (left.astype(F32) + right.astype(F32)).astype(BF16)

    def core_step(a, k):
        yy, zz = where(k)
        loads[a * chunks + k].wait()
        arrived(come.at[a, yy, zz], a, base["c"] + k)
        stay[a, yy, zz] = plus(stay[a, yy, zz], come[a, yy, zz])
        if k < groups:
            go(stay.at[a, yy, zz, rows_b], ybin.at[a, zz], *sems(a, base["yb"] + k), ypeer)
        for j in range(1, pipes):
            to = (p + j) % pipes
            cols = pl.ds(pl.multiple_of(to * share, 128), share)
            go(stay.at[a, yy, zz, rows_a, cols], xain.at[a, j - 1, yy, zz],
               *sems(a, base["xa"] + (j - 1) * chunks + k), peer(pipe=to))

    def xa_step(a, k):
        yy, zz = where(k)
        total = stay[a, yy, zz, rows_a, mine].astype(F32)
        for j in range(1, pipes):
            arrived(xain.at[a, j - 1, yy, zz], a, base["xa"] + (j - 1) * chunks + k)
            total = total + xain[a, j - 1, yy, zz].astype(F32)
        half[a, yy, zz] = total.astype(BF16)
        if k < groups:
            go(half.at[a, yy, zz], yain.at[a, zz], *sems(a, base["ya"] + k), ypeer)

    def yb_step(a, k):
        yy, zz = where(groups + k)
        arrived(ybin.at[a, zz], a, base["yb"] + k)
        mid[a, zz] = plus(stay[a, yy, zz, rows_b], ybin[a, zz])
        for j in range(1, pipes):
            to = (p + j) % pipes
            cols = pl.ds(pl.multiple_of(to * share, 128), share)
            go(mid.at[a, zz, :, cols], xbin.at[a, j - 1, zz],
               *sems(a, base["xb"] + (j - 1) * groups + k), peer(pipe=to))

    def z_send(a, h, d):
        to = (z + d) % outer
        go(line.at[a, h, to], zin.at[a, h, d - 1], *sems(a, base["zb" if h else "za"] + d - 1),
           peer(expert=join(to, y, c)))

    def line_done(a, h, k):
        if size == 1:
            if k < groups - 1:
                z_send(a, h, k + 1)
        elif k == groups - 1:
            for d in range(1, outer):
                z_send(a, h, d)

    def ya_step(a, k):
        yy, zz = where(groups + k)
        arrived(yain.at[a, zz], a, base["ya"] + k)
        line[a, 0, zz] = plus(half[a, yy, zz], yain[a, zz])
        line_done(a, 0, k)

    def xb_step(a, k):
        _, zz = where(k)
        total = mid[a, zz, :, mine].astype(F32)
        for j in range(1, pipes):
            arrived(xbin.at[a, j - 1, zz], a, base["xb"] + (j - 1) * groups + k)
            total = total + xbin[a, j - 1, zz].astype(F32)
        line[a, 1, zz] = total.astype(BF16)
        line_done(a, 1, k)

    def gate_step():
        for d in range(1, experts):
            b = (me + experts - d) % experts
            remote(gin.at[b], gin.at[b], gsend.at[d - 1], grecv.at[d - 1], cpeer).wait_recv()
        keep.wait()
        for j in range(1, pipes):
            go(gin, gx.at[j - 1], gxs.at[j - 1], gxr.at[j - 1], peer(pipe=(p + j) % pipes))

    for a in range(2):
        for k in range(chunks):
            core_step(a, k)
    for a in range(2):
        for k in range(groups):
            xa_step(a, k)
            yb_step(a, k)
        for k in range(groups):
            xa_step(a, groups + k)
            ya_step(a, k)
            xb_step(a, k)
        if a == 0:
            gate_step()
    whole = gin[...]
    for j in range(1, pipes):
        remote(gin, gx.at[j - 1], gxs.at[j - 1], gxr.at[j - 1], cpeer).wait_recv()
        whole = whole + gx[j - 1]
    ogate[...] = whole
    for a in range(2):
        for h in range(2):
            total = line[a, h, z].astype(F32)
            for d in range(1, outer):
                arrived(zin.at[a, h, d - 1], a, base["zb" if h else "za"] + d - 1)
                total = total + zin[a, h, d - 1].astype(F32)
            outs[a][h * top:(h + 1) * top] = total.astype(BF16)
    for copy in sent:
        copy.wait_send()


def reduce_all(pipes, experts, mixed, grad, gate):
    outer, groups, base, count = reduce_plan(pipes, experts)
    rows, width = mixed.shape[1:]
    share = width // pipes
    top = rows // 2
    shape = (outer, INNER, INNER, rows, width)
    hbm = pl.BlockSpec(memory_space=pl.ANY)
    vmem = pl.BlockSpec(memory_space=pltpu.VMEM)
    return pl.pallas_call(
        functools.partial(reduce_kernel, pipes, experts),
        out_shape=[jax.ShapeDtypeStruct((rows, share), BF16)] * 2
        + [jax.ShapeDtypeStruct(gate.shape, F32)],
        in_specs=[hbm, hbm, vmem],
        out_specs=[vmem] * 3,
        scratch_shapes=[
            pltpu.VMEM((2, INNER, outer, rows, width), BF16),
            pltpu.VMEM((2, INNER, outer, rows, width), BF16),
            pltpu.VMEM((2, pipes - 1, INNER, outer, top, share), BF16),
            pltpu.VMEM((2, INNER, outer, top, share), BF16),
            pltpu.VMEM((2, outer, top, share), BF16),
            pltpu.VMEM((2, outer, top, width), BF16),
            pltpu.VMEM((2, outer, top, width), BF16),
            pltpu.VMEM((2, pipes - 1, outer, top, share), BF16),
            pltpu.VMEM((2, 2, outer, top, share), BF16),
            pltpu.VMEM((2, 2, outer - 1, top, share), BF16),
            pltpu.VMEM(gate.shape, F32),
            pltpu.VMEM((pipes - 1,) + gate.shape, F32),
            pltpu.SemaphoreType.DMA((2 * count,)),
            pltpu.SemaphoreType.DMA((2 * count,)),
            pltpu.SemaphoreType.DMA((experts - 1,)),
            pltpu.SemaphoreType.DMA((experts - 1,)),
            pltpu.SemaphoreType.DMA((pipes - 1,)),
            pltpu.SemaphoreType.DMA((pipes - 1,)),
            pltpu.SemaphoreType.DMA((4 * groups + 1,)),
        ],
        compiler_params=pltpu.CompilerParams(collective_id=1, has_side_effects=True),
        name="reduce_rows",
    )(mixed.reshape(shape), grad.reshape(shape), gate)


def body(tokens, out_grad, routes, slots, gates, w_gate, w_up, w_down):
    local_tokens, topk = routes.shape
    pipes = lax.axis_size("pipe")
    experts = lax.axis_size("expert")
    capacity = 4 * local_tokens * topk // (3 * experts)
    width = tokens.shape[1]
    half = (topk + 7) // 8 * 8
    position = (routes * capacity + slots).astype(F32)
    pad = jnp.zeros((local_tokens, half - topk), F32)
    meta = jnp.concatenate([position, pad, gates.astype(F32), pad], axis=1).T
    xg, dyg, mg = gather_all(pipes, experts, tokens, out_grad, meta)

    rows = experts * capacity
    first = lax.axis_index("expert") * capacity
    wanted = (first + jnp.arange(capacity)).astype(F32)
    hit = mg[:, :topk, None, :] == wanted[None, None, :, None]
    pick = jnp.sum(hit.astype(F32), axis=1).astype(BF16)
    weigh = jnp.sum(jnp.where(hit, mg[:, half:half + topk, None, :], 0.0), axis=1).astype(BF16)
    by_token = (((2,), (1,)), ((0,), (0,)))

    def select(matrix, source):
        picked = lax.dot_general(matrix, source, by_token, preferred_element_type=F32)
        return picked.astype(BF16).reshape(rows, width)

    x = select(pick, xg)
    dy = select(pick, dyg)
    d_out = select(weigh, dyg)
    gate_w, up_w, down_w = w_gate[0], w_up[0], w_down[0]
    contract = (((1,), (1,)), ((), ()))
    over_rows = (((0,), (0,)), ((), ()))
    dot = functools.partial(lax.dot_general, preferred_element_type=F32)
    plain = (((1,), (0,)), ((), ()))
    gate_pre = dot(x, gate_w, contract)
    up_pre = dot(x, up_w, contract)
    sigma = jax.nn.sigmoid(gate_pre)
    silu_val = gate_pre * sigma
    act = (silu_val * up_pre).astype(BF16)
    partial_out = dot(act, down_w, plain).astype(BF16)
    d_act = dot(d_out, down_w, contract)
    d_gate = (d_act * up_pre * sigma * (1.0 + gate_pre * (1.0 - sigma))).astype(BF16)
    d_up = (d_act * silu_val).astype(BF16)
    partial_back = (dot(d_gate, gate_w, plain) + dot(d_up, up_w, plain)).astype(BF16)
    grad_gate_w = dot(d_gate, x, over_rows).astype(BF16)
    grad_up_w = dot(d_up, x, over_rows).astype(BF16)
    grad_down_w = dot(act, d_out, over_rows).astype(BF16)

    over_slots = (((1,), (1,)), ((0,), (0,)))
    shape = (experts, capacity, width)
    mixed_part = dot(weigh, partial_out.reshape(shape), over_slots).astype(BF16)
    grad_part = dot(pick, partial_back.reshape(shape), over_slots).astype(BF16)
    row_gate = jnp.sum(dy.astype(F32) * partial_out.astype(F32), axis=1).reshape(experts, capacity)
    gate_part = jnp.sum(pick.astype(F32) * row_gate[:, :, None], axis=1)
    gate_part = jnp.broadcast_to(gate_part[:, None, :], (experts, 8, local_tokens))
    mixed, grad_total, gate_all = reduce_all(pipes, experts, mixed_part, grad_part, gate_part)
    named = routes[:, :, None] == jnp.arange(experts)[None, None, :]
    grad_gates = jnp.sum(jnp.where(named, gate_all[:, 0, :].T[:, None, :], 0.0), axis=2)
    return (mixed, grad_total, grad_gates, grad_gate_w[None], grad_up_w[None], grad_down_w[None])


def solution(mesh):
    rows = P("expert", None)
    weights = P("expert", "pipe", None)
    return jax.shard_map(
        body,
        mesh=mesh,
        in_specs=(rows,) * 5 + (weights,) * 3,
        out_specs=(P("expert", "pipe"), P("expert", "pipe"), rows) + (weights,) * 3,
        check_vma=False,
    )
```

```python
import functools

import jax
import jax.numpy as jnp
from jax import lax
from jax.experimental import pallas as pl
from jax.experimental.pallas import tpu as pltpu
from jax.sharding import PartitionSpec as P

INNER = 2
BF16 = jnp.bfloat16
F32 = jnp.float32


def place(experts):
    me = lax.axis_index("expert")
    return me, me // (INNER * INNER), (me // INNER) % INNER, me % INNER


def join(outer, mid, low):
    return (outer * INNER + mid) * INNER + low


def peer(expert=None, pipe=None):
    p = lax.axis_index("pipe") if pipe is None else pipe
    e = lax.axis_index("expert") if expert is None else expert
    return (p, e)


def meet(pipes, experts):
    p = lax.axis_index("pipe")
    e = lax.axis_index("expert")
    barrier = pltpu.get_barrier_semaphore()
    for d in range(1, experts):
        pl.semaphore_signal(barrier, inc=1, device_id=peer(expert=(e + d) % experts),
                            device_id_type=pl.DeviceIdType.MESH)
    for d in range(1, pipes):
        pl.semaphore_signal(barrier, inc=1, device_id=peer(pipe=(p + d) % pipes),
                            device_id_type=pl.DeviceIdType.MESH)
    pl.semaphore_wait(barrier, experts + pipes - 2)


def remote(src, dst, send, recv, dev):
    return pltpu.make_async_remote_copy(src_ref=src, dst_ref=dst, send_sem=send, recv_sem=recv,
                                        device_id=dev, device_id_type=pl.DeviceIdType.MESH)


def gather_plan(pipes, experts):
    outer = experts // (INNER * INNER)
    lanes = 2 * outer - 1
    base = {"z": 0, "y": outer - 1, "own": 2 * outer - 1, "c": 2 * outer, "x": 2 * outer + lanes}
    base["cx"] = base["x"] + lanes
    base["down"] = base["cx"] + lanes
    return outer, lanes, base, base["down"] + outer - 1


def gather_kernel(pipes, experts, x, dy, meta, xg, dyg, mg, send, recv, msend, mrecv, local):
    me, z, y, c = place(experts)
    p = lax.axis_index("pipe")
    outer, lanes, base, count = gather_plan(pipes, experts)
    width = x.shape[1]
    side = (width // 128 * 3 // 8) * 128
    par = p % 2
    wide = pl.ds(pl.multiple_of(par * side, 128), width - side)
    give = pl.ds(pl.multiple_of(par * (width - side), 128), side)
    take = pl.ds(pl.multiple_of((1 - par) * (width - side), 128), side)
    xpeer = peer(pipe=p + 1 - 2 * par)
    cpeer = peer(expert=join(z, y, 1 - c))
    ypeer = peer(expert=join(z, 1 - y, c))
    own = [pltpu.make_async_copy(s, g.at[me], local.at[i])
           for i, (s, g) in enumerate(((x, xg), (dy, dyg), (meta, mg)))]
    for copy in own:
        copy.start()
    meet(pipes, experts)
    sent = []

    def go(src, dst, s, r, dev):
        copy = remote(src, dst, s, r, dev)
        copy.start()
        sent.append(copy)

    for d in range(1, experts):
        go(meta, mg.at[me], msend.at[d - 1], mrecv.at[d - 1], peer(expert=(me + d) % experts))
    arrays = ((x, xg), (dy, dyg))
    inner = jnp.minimum(z, outer - 1 - z)
    below_more = z > outer - 1 - z

    def nearest(n):
        paired = n < 2 * inner
        below = jnp.where(paired, n % 2 == 0, below_more)
        far = jnp.where(paired, n // 2 + 1, n - inner + 1)
        return below, jnp.where(below, far, outer - far)

    def sems(a, i):
        return send.at[a * count + i], recv.at[a * count + i]

    def arrived(ref, a, i):
        remote(ref, ref, *sems(a, i), cpeer).wait_recv()

    later = []

    def chain(src, block, a, up, down, slot_up, slot_down, dev_up, dev_down):
        g = arrays[a][1]
        for way, go_there, slot, dev in (("z", up, slot_up, dev_up),
                                         ("down", down, slot_down, dev_down)):
            copy = remote(src, g.at[block, :, wide], send.at[a * count + base[way] + slot - 1],
                          recv.at[a * count + base["z"] + slot - 1], dev)
            pl.when(go_there)(copy.start)
            later.append((go_there, copy))

    above = peer(expert=join(jnp.minimum(z + 1, outer - 1), y, c))
    under = peer(expert=join(jnp.maximum(z - 1, 0), y, c))

    def start(a):
        s, g = arrays[a]
        chain(s.at[:, wide], me, a, z < outer - 1, z > 0, 1, outer - 1, above, under)
        go(s.at[:, wide], g.at[me, :, wide], *sems(a, base["y"]), ypeer)
        go(s, g.at[me], *sems(a, base["own"]), cpeer)

    def z_event(a, n):
        g = arrays[a][1]
        below, d = nearest(n)
        b = join((z + outer - d) % outer, y, c)
        ref = g.at[b, :, wide]
        arrived(ref, a, base["z"] + d - 1)
        chain(ref, b, a, below & (z < outer - 1), jnp.logical_not(below) & (z > 0),
              jnp.minimum(d + 1, outer - 1), jnp.maximum(d - 1, 1), above, under)
        go(ref, ref, *sems(a, base["y"] + d), ypeer)
        go(g.at[b, :, give], g.at[b, :, give], *sems(a, base["x"] + d - 1), xpeer)
        go(ref, ref, *sems(a, base["c"] + d - 1), cpeer)

    def y_event(a, n):
        g = arrays[a][1]
        d = 0 if n < 0 else nearest(n)[1]
        b = join((z + outer - d) % outer, 1 - y, c)
        ref = g.at[b, :, wide]
        arrived(ref, a, base["y"] + d)
        go(g.at[b, :, give], g.at[b, :, give], *sems(a, base["x"] + outer - 1 + d), xpeer)
        go(ref, ref, *sems(a, base["c"] + outer - 1 + d), cpeer)

    def x_event(a, n, across):
        g = arrays[a][1]
        d = 0 if n < 0 else nearest(n)[1]
        b = join((z + outer - d) % outer, 1 - y if across else y, c)
        i = outer - 1 + d if across else d - 1
        arrived(g.at[b, :, take], a, base["x"] + i)
        go(g.at[b, :, take], g.at[b, :, take], *sems(a, base["cx"] + i), cpeer)

    steps = []
    for a in range(2):
        at = (outer + 0.2) * a
        steps += [(0.5, start, (a,))] if a else []
        steps += [(at + 2 * n, z_event, (a, n)) for n in range(outer - 1)]
        steps += [(at + 2 * n + 3, y_event, (a, n)) for n in range(-1, outer - 1)]
        steps += [(at + 2 * n + 9, x_event, (a, n, False)) for n in range(outer - 1)]
        steps += [(at + 2 * n + 11, x_event, (a, n, True)) for n in range(-1, outer - 1)]
    start(0)
    for _, run, args in sorted(steps, key=lambda step: step[0]):
        run(*args)
    for a, (s, g) in enumerate(arrays):
        arrived(g.at[join(z, y, 1 - c)], a, base["own"])
        for i in range(lanes):
            b = (join((z + outer - i - 1) % outer, y, 1 - c) if i < outer - 1
                 else join((z + outer - (i - outer + 1)) % outer, 1 - y, 1 - c))
            arrived(g.at[b, :, wide], a, base["c"] + i)
            arrived(g.at[b, :, take], a, base["cx"] + i)
    for go_there, copy in later:
        pl.when(go_there)(copy.wait_send)
    for d in range(1, experts):
        b = (me + experts - d) % experts
        remote(mg.at[b], mg.at[b], msend.at[d - 1], mrecv.at[d - 1], cpeer).wait_recv()
    for copy in sent:
        copy.wait_send()
    for copy in own:
        copy.wait()


def gather_all(pipes, experts, x, dy, meta):
    count = gather_plan(pipes, experts)[3]
    hbm = pl.BlockSpec(memory_space=pl.ANY)
    vmem = pl.BlockSpec(memory_space=pltpu.VMEM)
    return pl.pallas_call(
        functools.partial(gather_kernel, pipes, experts),
        out_shape=[jax.ShapeDtypeStruct((experts,) + v.shape, v.dtype) for v in (x, dy, meta)],
        in_specs=[vmem] * 3,
        out_specs=[hbm] * 3,
        scratch_shapes=[
            pltpu.SemaphoreType.DMA((2 * count,)),
            pltpu.SemaphoreType.DMA((2 * count,)),
            pltpu.SemaphoreType.DMA((experts - 1,)),
            pltpu.SemaphoreType.DMA((experts - 1,)),
            pltpu.SemaphoreType.DMA((3,)),
        ],
        compiler_params=pltpu.CompilerParams(collective_id=0, has_side_effects=True),
        name="gather_rows",
    )(x, dy, meta)


def reduce_plan(pipes, experts):
    outer = experts // (INNER * INNER)
    groups = min(outer, 4)
    chunks = 2 * groups
    sizes = (("c", chunks), ("xa", chunks * (pipes - 1)), ("ya", groups), ("yb", groups),
             ("xb", groups * (pipes - 1)), ("za", outer - 1), ("zb", outer - 1))
    base, total = {}, 0
    for name, size in sizes:
        base[name] = total
        total += size
    return outer, groups, base, total


def reduce_kernel(pipes, experts, pm, pg, gate, om, og, ogate,
                  stay, come, xain, half, yain, ybin, mid, xbin, line, zin, gin, gx,
                  send, recv, gsend, grecv, gxs, gxr, local):
    me, z, y, c = place(experts)
    p = lax.axis_index("pipe")
    outer, groups, base, count = reduce_plan(pipes, experts)
    size = outer // groups
    chunks = 2 * groups
    share = om.shape[1]
    top = om.shape[0] // 2
    rows_a, rows_b = pl.ds(0, top), pl.ds(top, top)
    cpeer = peer(expert=join(z, y, 1 - c))
    ypeer = peer(expert=join(z, 1 - y, c))
    mine = pl.ds(pl.multiple_of(p * share, 128), share)
    parts = (pm, pg)
    outs = (om, og)

    def where(k):
        g = (z // size + 1 + k % groups) % groups
        return (y + 1 + k // groups) % 2, pl.ds(g * size, size)

    loads = []
    for a in range(2):
        for k in range(chunks):
            yy, zz = where(k)
            copy = pltpu.make_async_copy(parts[a].at[zz, yy, c], stay.at[a, yy, zz],
                                         local.at[a * chunks + k])
            copy.start()
            loads.append(copy)
    keep = pltpu.make_async_copy(gate.at[me], gin.at[me], local.at[2 * chunks])
    keep.start()
    meet(pipes, experts)
    sent = []

    def sems(a, i):
        return send.at[a * count + i], recv.at[a * count + i]

    def go(src, dst, s, r, dev):
        copy = remote(src, dst, s, r, dev)
        copy.start()
        sent.append(copy)

    def arrived(ref, a, i):
        remote(ref, ref, *sems(a, i), cpeer).wait_recv()

    for d in range(1, experts):
        to = (me + d) % experts
        go(gate.at[to], gin.at[me], gsend.at[d - 1], grecv.at[d - 1], peer(expert=to))
    for a in range(2):
        for k in range(chunks):
            yy, zz = where(k)
            go(parts[a].at[zz, yy, 1 - c], come.at[a, yy, zz], *sems(a, base["c"] + k), cpeer)

    def plus(left, right):
        return (left.astype(F32) + right.astype(F32)).astype(BF16)

    def core_step(a, k):
        yy, zz = where(k)
        loads[a * chunks + k].wait()
        arrived(come.at[a, yy, zz], a, base["c"] + k)
        stay[a, yy, zz] = plus(stay[a, yy, zz], come[a, yy, zz])
        if k < groups:
            go(stay.at[a, yy, zz, rows_b], ybin.at[a, zz], *sems(a, base["yb"] + k), ypeer)
        for j in range(1, pipes):
            to = (p + j) % pipes
            cols = pl.ds(pl.multiple_of(to * share, 128), share)
            go(stay.at[a, yy, zz, rows_a, cols], xain.at[a, j - 1, yy, zz],
               *sems(a, base["xa"] + (j - 1) * chunks + k), peer(pipe=to))

    def xa_step(a, k):
        yy, zz = where(k)
        total = stay[a, yy, zz, rows_a, mine].astype(F32)
        for j in range(1, pipes):
            arrived(xain.at[a, j - 1, yy, zz], a, base["xa"] + (j - 1) * chunks + k)
            total = total + xain[a, j - 1, yy, zz].astype(F32)
        half[a, yy, zz] = total.astype(BF16)
        if k < groups:
            go(half.at[a, yy, zz], yain.at[a, zz], *sems(a, base["ya"] + k), ypeer)

    def yb_step(a, k):
        yy, zz = where(groups + k)
        arrived(ybin.at[a, zz], a, base["yb"] + k)
        mid[a, zz] = plus(stay[a, yy, zz, rows_b], ybin[a, zz])
        for j in range(1, pipes):
            to = (p + j) % pipes
            cols = pl.ds(pl.multiple_of(to * share, 128), share)
            go(mid.at[a, zz, :, cols], xbin.at[a, j - 1, zz],
               *sems(a, base["xb"] + (j - 1) * groups + k), peer(pipe=to))

    def z_send(a, h, d):
        to = (z + d) % outer
        go(line.at[a, h, to], zin.at[a, h, d - 1], *sems(a, base["zb" if h else "za"] + d - 1),
           peer(expert=join(to, y, c)))

    def line_done(a, h, k):
        if size == 1:
            if k < groups - 1:
                z_send(a, h, k + 1)
        elif k == groups - 1:
            for d in range(1, outer):
                z_send(a, h, d)

    def ya_step(a, k):
        yy, zz = where(groups + k)
        arrived(yain.at[a, zz], a, base["ya"] + k)
        line[a, 0, zz] = plus(half[a, yy, zz], yain[a, zz])
        line_done(a, 0, k)

    def xb_step(a, k):
        _, zz = where(k)
        total = mid[a, zz, :, mine].astype(F32)
        for j in range(1, pipes):
            arrived(xbin.at[a, j - 1, zz], a, base["xb"] + (j - 1) * groups + k)
            total = total + xbin[a, j - 1, zz].astype(F32)
        line[a, 1, zz] = total.astype(BF16)
        line_done(a, 1, k)

    def gate_step():
        for d in range(1, experts):
            b = (me + experts - d) % experts
            remote(gin.at[b], gin.at[b], gsend.at[d - 1], grecv.at[d - 1], cpeer).wait_recv()
        keep.wait()
        for j in range(1, pipes):
            go(gin, gx.at[j - 1], gxs.at[j - 1], gxr.at[j - 1], peer(pipe=(p + j) % pipes))

    def first_hops(a):
        for k in range(groups):
            xa_step(a, k)
            yb_step(a, k)

    def last_hops(a):
        for k in range(groups):
            xa_step(a, groups + k)
            ya_step(a, k)
            xb_step(a, k)

    for k in range(chunks):
        core_step(0, k)
    first_hops(0)
    for k in range(chunks):
        core_step(1, k)
    last_hops(0)
    gate_step()
    first_hops(1)
    last_hops(1)
    whole = gin[...]
    for j in range(1, pipes):
        remote(gin, gx.at[j - 1], gxs.at[j - 1], gxr.at[j - 1], cpeer).wait_recv()
        whole = whole + gx[j - 1]
    ogate[...] = whole
    for a in range(2):
        for h in range(2):
            total = line[a, h, z].astype(F32)
            for d in range(1, outer):
                arrived(zin.at[a, h, d - 1], a, base["zb" if h else "za"] + d - 1)
                total = total + zin[a, h, d - 1].astype(F32)
            outs[a][h * top:(h + 1) * top] = total.astype(BF16)
    for copy in sent:
        copy.wait_send()


def reduce_all(pipes, experts, mixed, grad, gate):
    outer, groups, base, count = reduce_plan(pipes, experts)
    rows, width = mixed.shape[1:]
    share = width // pipes
    top = rows // 2
    shape = (outer, INNER, INNER, rows, width)
    hbm = pl.BlockSpec(memory_space=pl.ANY)
    vmem = pl.BlockSpec(memory_space=pltpu.VMEM)
    return pl.pallas_call(
        functools.partial(reduce_kernel, pipes, experts),
        out_shape=[jax.ShapeDtypeStruct((rows, share), BF16)] * 2
        + [jax.ShapeDtypeStruct(gate.shape, F32)],
        in_specs=[hbm, hbm, vmem],
        out_specs=[vmem] * 3,
        scratch_shapes=[
            pltpu.VMEM((2, INNER, outer, rows, width), BF16),
            pltpu.VMEM((2, INNER, outer, rows, width), BF16),
            pltpu.VMEM((2, pipes - 1, INNER, outer, top, share), BF16),
            pltpu.VMEM((2, INNER, outer, top, share), BF16),
            pltpu.VMEM((2, outer, top, share), BF16),
            pltpu.VMEM((2, outer, top, width), BF16),
            pltpu.VMEM((2, outer, top, width), BF16),
            pltpu.VMEM((2, pipes - 1, outer, top, share), BF16),
            pltpu.VMEM((2, 2, outer, top, share), BF16),
            pltpu.VMEM((2, 2, outer - 1, top, share), BF16),
            pltpu.VMEM(gate.shape, F32),
            pltpu.VMEM((pipes - 1,) + gate.shape, F32),
            pltpu.SemaphoreType.DMA((2 * count,)),
            pltpu.SemaphoreType.DMA((2 * count,)),
            pltpu.SemaphoreType.DMA((experts - 1,)),
            pltpu.SemaphoreType.DMA((experts - 1,)),
            pltpu.SemaphoreType.DMA((pipes - 1,)),
            pltpu.SemaphoreType.DMA((pipes - 1,)),
            pltpu.SemaphoreType.DMA((4 * groups + 1,)),
        ],
        compiler_params=pltpu.CompilerParams(collective_id=1, has_side_effects=True),
        name="reduce_rows",
    )(mixed.reshape(shape), grad.reshape(shape), gate)


def body(tokens, out_grad, routes, slots, gates, w_gate, w_up, w_down):
    local_tokens, topk = routes.shape
    pipes = lax.axis_size("pipe")
    experts = lax.axis_size("expert")
    capacity = 4 * local_tokens * topk // (3 * experts)
    width = tokens.shape[1]
    half = (topk + 7) // 8 * 8
    position = (routes * capacity + slots).astype(F32)
    pad = jnp.zeros((local_tokens, half - topk), F32)
    meta = jnp.concatenate([position, pad, gates.astype(F32), pad], axis=1).T
    xg, dyg, mg = gather_all(pipes, experts, tokens, out_grad, meta)

    rows = experts * capacity
    first = lax.axis_index("expert") * capacity
    wanted = (first + jnp.arange(capacity)).astype(F32)
    hit = mg[:, :topk, None, :] == wanted[None, None, :, None]
    pick = jnp.sum(hit.astype(F32), axis=1).astype(BF16)
    weigh = jnp.sum(jnp.where(hit, mg[:, half:half + topk, None, :], 0.0), axis=1).astype(BF16)
    by_token = (((2,), (1,)), ((0,), (0,)))

    def select(matrix, source):
        picked = lax.dot_general(matrix, source, by_token, preferred_element_type=F32)
        return picked.astype(BF16).reshape(rows, width)

    x = select(pick, xg)
    dy = select(pick, dyg)
    d_out = select(weigh, dyg)
    gate_w, up_w, down_w = w_gate[0], w_up[0], w_down[0]
    contract = (((1,), (1,)), ((), ()))
    over_rows = (((0,), (0,)), ((), ()))
    dot = functools.partial(lax.dot_general, preferred_element_type=F32)
    plain = (((1,), (0,)), ((), ()))
    gate_pre = dot(x, gate_w, contract)
    up_pre = dot(x, up_w, contract)
    sigma = jax.nn.sigmoid(gate_pre)
    silu_val = gate_pre * sigma
    act = (silu_val * up_pre).astype(BF16)
    partial_out = dot(act, down_w, plain).astype(BF16)
    d_act = dot(d_out, down_w, contract)
    d_gate = (d_act * up_pre * sigma * (1.0 + gate_pre * (1.0 - sigma))).astype(BF16)
    d_up = (d_act * silu_val).astype(BF16)
    partial_back = (dot(d_gate, gate_w, plain) + dot(d_up, up_w, plain)).astype(BF16)
    grad_gate_w = dot(d_gate, x, over_rows).astype(BF16)
    grad_up_w = dot(d_up, x, over_rows).astype(BF16)
    grad_down_w = dot(act, d_out, over_rows).astype(BF16)

    over_slots = (((1,), (1,)), ((0,), (0,)))
    shape = (experts, capacity, width)
    mixed_part = dot(weigh, partial_out.reshape(shape), over_slots).astype(BF16)
    grad_part = dot(pick, partial_back.reshape(shape), over_slots).astype(BF16)
    row_gate = jnp.sum(dy.astype(F32) * partial_out.astype(F32), axis=1).reshape(experts, capacity)
    gate_part = jnp.sum(pick.astype(F32) * row_gate[:, :, None], axis=1)
    gate_part = jnp.broadcast_to(gate_part[:, None, :], (experts, 8, local_tokens))
    mixed, grad_total, gate_all = reduce_all(pipes, experts, mixed_part, grad_part, gate_part)
    named = routes[:, :, None] == jnp.arange(experts)[None, None, :]
    grad_gates = jnp.sum(jnp.where(named, gate_all[:, 0, :].T[:, None, :], 0.0), axis=2)
    return (mixed, grad_total, grad_gates, grad_gate_w[None], grad_up_w[None], grad_down_w[None])


def solution(mesh):
    rows = P("expert", None)
    weights = P("expert", "pipe", None)
    return jax.shard_map(
        body,
        mesh=mesh,
        in_specs=(rows,) * 5 + (weights,) * 3,
        out_specs=(P("expert", "pipe"), P("expert", "pipe"), rows) + (weights,) * 3,
        check_vma=False,
    )
```

```python
import functools

import jax
import jax.numpy as jnp
from jax import lax
from jax.experimental import pallas as pl
from jax.experimental.pallas import tpu as pltpu
from jax.sharding import PartitionSpec as P

INNER = 2
BF16 = jnp.bfloat16
F32 = jnp.float32


def place(experts):
    me = lax.axis_index("expert")
    return me, me // (INNER * INNER), (me // INNER) % INNER, me % INNER


def join(outer, mid, low):
    return (outer * INNER + mid) * INNER + low


def peer(expert=None, pipe=None):
    p = lax.axis_index("pipe") if pipe is None else pipe
    e = lax.axis_index("expert") if expert is None else expert
    return (p, e)


def meet(pipes, experts):
    p = lax.axis_index("pipe")
    e = lax.axis_index("expert")
    barrier = pltpu.get_barrier_semaphore()
    for d in range(1, experts):
        pl.semaphore_signal(barrier, inc=1, device_id=peer(expert=(e + d) % experts),
                            device_id_type=pl.DeviceIdType.MESH)
    for d in range(1, pipes):
        pl.semaphore_signal(barrier, inc=1, device_id=peer(pipe=(p + d) % pipes),
                            device_id_type=pl.DeviceIdType.MESH)
    pl.semaphore_wait(barrier, experts + pipes - 2)


def remote(src, dst, send, recv, dev):
    return pltpu.make_async_remote_copy(src_ref=src, dst_ref=dst, send_sem=send, recv_sem=recv,
                                        device_id=dev, device_id_type=pl.DeviceIdType.MESH)


def gather_plan(pipes, experts):
    outer = experts // (INNER * INNER)
    lanes = 2 * outer - 1
    base = {"z": 0, "y": outer - 1, "own": 2 * outer - 1, "c": 2 * outer, "x": 2 * outer + lanes}
    base["cx"] = base["x"] + lanes
    base["down"] = base["cx"] + lanes
    return outer, lanes, base, base["down"] + outer - 1


def gather_kernel(pipes, experts, x, dy, meta, xg, dyg, mg, send, recv, msend, mrecv, local):
    me, z, y, c = place(experts)
    p = lax.axis_index("pipe")
    outer, lanes, base, count = gather_plan(pipes, experts)
    width = x.shape[1]
    side = (width // 128 * 3 // 8) * 128
    par = p % 2
    wide = pl.ds(pl.multiple_of(par * side, 128), width - side)
    give = pl.ds(pl.multiple_of(par * (width - side), 128), side)
    take = pl.ds(pl.multiple_of((1 - par) * (width - side), 128), side)
    xpeer = peer(pipe=p + 1 - 2 * par)
    cpeer = peer(expert=join(z, y, 1 - c))
    ypeer = peer(expert=join(z, 1 - y, c))
    own = [pltpu.make_async_copy(s, g.at[me], local.at[i])
           for i, (s, g) in enumerate(((x, xg), (dy, dyg), (meta, mg)))]
    for copy in own:
        copy.start()
    meet(pipes, experts)
    sent = []

    def go(src, dst, s, r, dev):
        copy = remote(src, dst, s, r, dev)
        copy.start()
        sent.append(copy)

    arrays = ((x, xg), (dy, dyg))
    inner = jnp.minimum(z, outer - 1 - z)
    below_more = z > outer - 1 - z

    def nearest(n):
        paired = n < 2 * inner
        below = jnp.where(paired, n % 2 == 0, below_more)
        far = jnp.where(paired, n // 2 + 1, n - inner + 1)
        return below, jnp.where(below, far, outer - far)

    def sems(a, i):
        return send.at[a * count + i], recv.at[a * count + i]

    def arrived(ref, a, i):
        remote(ref, ref, *sems(a, i), cpeer).wait_recv()

    later = []

    def chain(src, block, a, up, down, slot_up, slot_down, dev_up, dev_down):
        g = arrays[a][1]
        for way, go_there, slot, dev in (("z", up, slot_up, dev_up),
                                         ("down", down, slot_down, dev_down)):
            copy = remote(src, g.at[block, :, wide], send.at[a * count + base[way] + slot - 1],
                          recv.at[a * count + base["z"] + slot - 1], dev)
            pl.when(go_there)(copy.start)
            later.append((go_there, copy))

    above = peer(expert=join(jnp.minimum(z + 1, outer - 1), y, c))
    under = peer(expert=join(jnp.maximum(z - 1, 0), y, c))

    def start(a):
        s, g = arrays[a]
        chain(s.at[:, wide], me, a, z < outer - 1, z > 0, 1, outer - 1, above, under)
        go(s.at[:, wide], g.at[me, :, wide], *sems(a, base["y"]), ypeer)
        go(s, g.at[me], *sems(a, base["own"]), cpeer)

    def z_event(a, n):
        g = arrays[a][1]
        below, d = nearest(n)
        b = join((z + outer - d) % outer, y, c)
        ref = g.at[b, :, wide]
        arrived(ref, a, base["z"] + d - 1)
        chain(ref, b, a, below & (z < outer - 1), jnp.logical_not(below) & (z > 0),
              jnp.minimum(d + 1, outer - 1), jnp.maximum(d - 1, 1), above, under)
        go(ref, ref, *sems(a, base["y"] + d), ypeer)
        go(g.at[b, :, give], g.at[b, :, give], *sems(a, base["x"] + d - 1), xpeer)
        go(ref, ref, *sems(a, base["c"] + d - 1), cpeer)

    def y_event(a, n):
        g = arrays[a][1]
        d = 0 if n < 0 else nearest(n)[1]
        b = join((z + outer - d) % outer, 1 - y, c)
        ref = g.at[b, :, wide]
        arrived(ref, a, base["y"] + d)
        go(g.at[b, :, give], g.at[b, :, give], *sems(a, base["x"] + outer - 1 + d), xpeer)
        go(ref, ref, *sems(a, base["c"] + outer - 1 + d), cpeer)

    def x_event(a, n, across):
        g = arrays[a][1]
        d = 0 if n < 0 else nearest(n)[1]
        b = join((z + outer - d) % outer, 1 - y if across else y, c)
        i = outer - 1 + d if across else d - 1
        arrived(g.at[b, :, take], a, base["x"] + i)
        go(g.at[b, :, take], g.at[b, :, take], *sems(a, base["cx"] + i), cpeer)

    steps = []
    for a in range(2):
        at = (outer + 0.2) * a
        steps += [(0.5, start, (a,))] if a else []
        steps += [(at + 2 * n, z_event, (a, n)) for n in range(outer - 1)]
        steps += [(at + 2 * n + 3, y_event, (a, n)) for n in range(-1, outer - 1)]
        steps += [(at + 2 * n + 9, x_event, (a, n, False)) for n in range(outer - 1)]
        steps += [(at + 2 * n + 11, x_event, (a, n, True)) for n in range(-1, outer - 1)]
    start(0)
    for d in range(1, experts):
        go(meta, mg.at[me], msend.at[d - 1], mrecv.at[d - 1], peer(expert=(me + d) % experts))
    for _, run, args in sorted(steps, key=lambda step: step[0]):
        run(*args)
    for a, (s, g) in enumerate(arrays):
        arrived(g.at[join(z, y, 1 - c)], a, base["own"])
        for i in range(lanes):
            b = (join((z + outer - i - 1) % outer, y, 1 - c) if i < outer - 1
                 else join((z + outer - (i - outer + 1)) % outer, 1 - y, 1 - c))
            arrived(g.at[b, :, wide], a, base["c"] + i)
            arrived(g.at[b, :, take], a, base["cx"] + i)
    for go_there, copy in later:
        pl.when(go_there)(copy.wait_send)
    for d in range(1, experts):
        b = (me + experts - d) % experts
        remote(mg.at[b], mg.at[b], msend.at[d - 1], mrecv.at[d - 1], cpeer).wait_recv()
    for copy in sent:
        copy.wait_send()
    for copy in own:
        copy.wait()


def gather_all(pipes, experts, x, dy, meta):
    count = gather_plan(pipes, experts)[3]
    hbm = pl.BlockSpec(memory_space=pl.ANY)
    vmem = pl.BlockSpec(memory_space=pltpu.VMEM)
    return pl.pallas_call(
        functools.partial(gather_kernel, pipes, experts),
        out_shape=[jax.ShapeDtypeStruct((experts,) + v.shape, v.dtype) for v in (x, dy, meta)],
        in_specs=[vmem] * 3,
        out_specs=[hbm] * 3,
        scratch_shapes=[
            pltpu.SemaphoreType.DMA((2 * count,)),
            pltpu.SemaphoreType.DMA((2 * count,)),
            pltpu.SemaphoreType.DMA((experts - 1,)),
            pltpu.SemaphoreType.DMA((experts - 1,)),
            pltpu.SemaphoreType.DMA((3,)),
        ],
        compiler_params=pltpu.CompilerParams(collective_id=0, has_side_effects=True),
        name="gather_rows",
    )(x, dy, meta)


def reduce_plan(pipes, experts):
    outer = experts // (INNER * INNER)
    groups = min(outer, 4)
    chunks = 2 * groups
    sizes = (("c", chunks), ("xa", chunks * (pipes - 1)), ("ya", groups), ("yb", groups),
             ("xb", groups * (pipes - 1)), ("za", outer - 1), ("zb", outer - 1))
    base, total = {}, 0
    for name, size in sizes:
        base[name] = total
        total += size
    return outer, groups, base, total


def reduce_kernel(pipes, experts, pm, pg, gate, om, og, ogate,
                  stay, come, xain, half, yain, ybin, mid, xbin, line, zin, gin, gx,
                  send, recv, gsend, grecv, gxs, gxr, local):
    me, z, y, c = place(experts)
    p = lax.axis_index("pipe")
    outer, groups, base, count = reduce_plan(pipes, experts)
    size = outer // groups
    chunks = 2 * groups
    share = om.shape[1]
    top = om.shape[0] // 2
    rows_a, rows_b = pl.ds(0, top), pl.ds(top, top)
    cpeer = peer(expert=join(z, y, 1 - c))
    ypeer = peer(expert=join(z, 1 - y, c))
    mine = pl.ds(pl.multiple_of(p * share, 128), share)
    parts = (pm, pg)
    outs = (om, og)

    def where(k):
        g = (z // size + 1 + k % groups) % groups
        return (y + 1 + k // groups) % 2, pl.ds(g * size, size)

    loads = []
    for a in range(2):
        for k in range(chunks):
            yy, zz = where(k)
            copy = pltpu.make_async_copy(parts[a].at[zz, yy, c], stay.at[a, yy, zz],
                                         local.at[a * chunks + k])
            copy.start()
            loads.append(copy)
    keep = pltpu.make_async_copy(gate.at[me], gin.at[me], local.at[2 * chunks])
    keep.start()
    meet(pipes, experts)
    sent = []

    def sems(a, i):
        return send.at[a * count + i], recv.at[a * count + i]

    def go(src, dst, s, r, dev):
        copy = remote(src, dst, s, r, dev)
        copy.start()
        sent.append(copy)

    def arrived(ref, a, i):
        remote(ref, ref, *sems(a, i), cpeer).wait_recv()

    for a in range(2):
        for k in range(chunks):
            yy, zz = where(k)
            go(parts[a].at[zz, yy, 1 - c], come.at[a, yy, zz], *sems(a, base["c"] + k), cpeer)

    def plus(left, right):
        return (left.astype(F32) + right.astype(F32)).astype(BF16)

    def core_step(a, k):
        yy, zz = where(k)
        loads[a * chunks + k].wait()
        arrived(come.at[a, yy, zz], a, base["c"] + k)
        stay[a, yy, zz] = plus(stay[a, yy, zz], come[a, yy, zz])
        if k < groups:
            go(stay.at[a, yy, zz, rows_b], ybin.at[a, zz], *sems(a, base["yb"] + k), ypeer)
        for j in range(1, pipes):
            to = (p + j) % pipes
            cols = pl.ds(pl.multiple_of(to * share, 128), share)
            go(stay.at[a, yy, zz, rows_a, cols], xain.at[a, j - 1, yy, zz],
               *sems(a, base["xa"] + (j - 1) * chunks + k), peer(pipe=to))

    def xa_step(a, k):
        yy, zz = where(k)
        total = stay[a, yy, zz, rows_a, mine].astype(F32)
        for j in range(1, pipes):
            arrived(xain.at[a, j - 1, yy, zz], a, base["xa"] + (j - 1) * chunks + k)
            total = total + xain[a, j - 1, yy, zz].astype(F32)
        half[a, yy, zz] = total.astype(BF16)
        if k < groups:
            go(half.at[a, yy, zz], yain.at[a, zz], *sems(a, base["ya"] + k), ypeer)

    def yb_step(a, k):
        yy, zz = where(groups + k)
        arrived(ybin.at[a, zz], a, base["yb"] + k)
        mid[a, zz] = plus(stay[a, yy, zz, rows_b], ybin[a, zz])
        for j in range(1, pipes):
            to = (p + j) % pipes
            cols = pl.ds(pl.multiple_of(to * share, 128), share)
            go(mid.at[a, zz, :, cols], xbin.at[a, j - 1, zz],
               *sems(a, base["xb"] + (j - 1) * groups + k), peer(pipe=to))

    def z_send(a, h, d):
        to = (z + d) % outer
        go(line.at[a, h, to], zin.at[a, h, d - 1], *sems(a, base["zb" if h else "za"] + d - 1),
           peer(expert=join(to, y, c)))

    def line_done(a, h, k):
        if size == 1:
            if k < groups - 1:
                z_send(a, h, k + 1)
        elif k == groups - 1:
            for d in range(1, outer):
                z_send(a, h, d)

    def ya_step(a, k):
        yy, zz = where(groups + k)
        arrived(yain.at[a, zz], a, base["ya"] + k)
        line[a, 0, zz] = plus(half[a, yy, zz], yain[a, zz])
        line_done(a, 0, k)

    def xb_step(a, k):
        _, zz = where(k)
        total = mid[a, zz, :, mine].astype(F32)
        for j in range(1, pipes):
            arrived(xbin.at[a, j - 1, zz], a, base["xb"] + (j - 1) * groups + k)
            total = total + xbin[a, j - 1, zz].astype(F32)
        line[a, 1, zz] = total.astype(BF16)
        line_done(a, 1, k)

    def gate_step():
        for d in range(1, experts):
            b = (me + experts - d) % experts
            remote(gin.at[b], gin.at[b], gsend.at[d - 1], grecv.at[d - 1], cpeer).wait_recv()
        keep.wait()
        for j in range(1, pipes):
            go(gin, gx.at[j - 1], gxs.at[j - 1], gxr.at[j - 1], peer(pipe=(p + j) % pipes))

    def first_hops(a):
        for k in range(groups):
            xa_step(a, k)
            yb_step(a, k)

    def last_hops(a):
        for k in range(groups):
            xa_step(a, groups + k)
            ya_step(a, k)
            xb_step(a, k)

    for k in range(chunks):
        core_step(0, k)
    for d in range(1, experts):
        to = (me + d) % experts
        go(gate.at[to], gin.at[me], gsend.at[d - 1], grecv.at[d - 1], peer(expert=to))
    first_hops(0)
    for k in range(chunks):
        core_step(1, k)
    last_hops(0)
    gate_step()
    first_hops(1)
    last_hops(1)
    whole = gin[...]
    for j in range(1, pipes):
        remote(gin, gx.at[j - 1], gxs.at[j - 1], gxr.at[j - 1], cpeer).wait_recv()
        whole = whole + gx[j - 1]
    ogate[...] = whole
    for a in range(2):
        for h in range(2):
            total = line[a, h, z].astype(F32)
            for d in range(1, outer):
                arrived(zin.at[a, h, d - 1], a, base["zb" if h else "za"] + d - 1)
                total = total + zin[a, h, d - 1].astype(F32)
            outs[a][h * top:(h + 1) * top] = total.astype(BF16)
    for copy in sent:
        copy.wait_send()


def reduce_all(pipes, experts, mixed, grad, gate):
    outer, groups, base, count = reduce_plan(pipes, experts)
    rows, width = mixed.shape[1:]
    share = width // pipes
    top = rows // 2
    shape = (outer, INNER, INNER, rows, width)
    hbm = pl.BlockSpec(memory_space=pl.ANY)
    vmem = pl.BlockSpec(memory_space=pltpu.VMEM)
    return pl.pallas_call(
        functools.partial(reduce_kernel, pipes, experts),
        out_shape=[jax.ShapeDtypeStruct((rows, share), BF16)] * 2
        + [jax.ShapeDtypeStruct(gate.shape, F32)],
        in_specs=[hbm, hbm, vmem],
        out_specs=[vmem] * 3,
        scratch_shapes=[
            pltpu.VMEM((2, INNER, outer, rows, width), BF16),
            pltpu.VMEM((2, INNER, outer, rows, width), BF16),
            pltpu.VMEM((2, pipes - 1, INNER, outer, top, share), BF16),
            pltpu.VMEM((2, INNER, outer, top, share), BF16),
            pltpu.VMEM((2, outer, top, share), BF16),
            pltpu.VMEM((2, outer, top, width), BF16),
            pltpu.VMEM((2, outer, top, width), BF16),
            pltpu.VMEM((2, pipes - 1, outer, top, share), BF16),
            pltpu.VMEM((2, 2, outer, top, share), BF16),
            pltpu.VMEM((2, 2, outer - 1, top, share), BF16),
            pltpu.VMEM(gate.shape, F32),
            pltpu.VMEM((pipes - 1,) + gate.shape, F32),
            pltpu.SemaphoreType.DMA((2 * count,)),
            pltpu.SemaphoreType.DMA((2 * count,)),
            pltpu.SemaphoreType.DMA((experts - 1,)),
            pltpu.SemaphoreType.DMA((experts - 1,)),
            pltpu.SemaphoreType.DMA((pipes - 1,)),
            pltpu.SemaphoreType.DMA((pipes - 1,)),
            pltpu.SemaphoreType.DMA((4 * groups + 1,)),
        ],
        compiler_params=pltpu.CompilerParams(collective_id=1, has_side_effects=True),
        name="reduce_rows",
    )(mixed.reshape(shape), grad.reshape(shape), gate)


def body(tokens, out_grad, routes, slots, gates, w_gate, w_up, w_down):
    local_tokens, topk = routes.shape
    pipes = lax.axis_size("pipe")
    experts = lax.axis_size("expert")
    capacity = 4 * local_tokens * topk // (3 * experts)
    width = tokens.shape[1]
    half = (topk + 7) // 8 * 8
    position = (routes * capacity + slots).astype(F32)
    pad = jnp.zeros((local_tokens, half - topk), F32)
    meta = jnp.concatenate([position, pad, gates.astype(F32), pad], axis=1).T
    xg, dyg, mg = gather_all(pipes, experts, tokens, out_grad, meta)

    rows = experts * capacity
    first = lax.axis_index("expert") * capacity
    wanted = (first + jnp.arange(capacity)).astype(F32)
    hit = mg[:, :topk, None, :] == wanted[None, None, :, None]
    pick = jnp.sum(hit.astype(F32), axis=1).astype(BF16)
    weigh = jnp.sum(jnp.where(hit, mg[:, half:half + topk, None, :], 0.0), axis=1).astype(BF16)
    by_token = (((2,), (1,)), ((0,), (0,)))

    def select(matrix, source):
        picked = lax.dot_general(matrix, source, by_token, preferred_element_type=F32)
        return picked.astype(BF16).reshape(rows, width)

    x = select(pick, xg)
    dy = select(pick, dyg)
    d_out = select(weigh, dyg)
    gate_w, up_w, down_w = w_gate[0], w_up[0], w_down[0]
    contract = (((1,), (1,)), ((), ()))
    over_rows = (((0,), (0,)), ((), ()))
    dot = functools.partial(lax.dot_general, preferred_element_type=F32)
    plain = (((1,), (0,)), ((), ()))
    gate_pre = dot(x, gate_w, contract)
    up_pre = dot(x, up_w, contract)
    sigma = jax.nn.sigmoid(gate_pre)
    silu_val = gate_pre * sigma
    act = (silu_val * up_pre).astype(BF16)
    partial_out = dot(act, down_w, plain).astype(BF16)
    d_act = dot(d_out, down_w, contract)
    d_gate = (d_act * up_pre * sigma * (1.0 + gate_pre * (1.0 - sigma))).astype(BF16)
    d_up = (d_act * silu_val).astype(BF16)
    partial_back = (dot(d_gate, gate_w, plain) + dot(d_up, up_w, plain)).astype(BF16)
    grad_gate_w = dot(d_gate, x, over_rows).astype(BF16)
    grad_up_w = dot(d_up, x, over_rows).astype(BF16)
    grad_down_w = dot(act, d_out, over_rows).astype(BF16)

    over_slots = (((1,), (1,)), ((0,), (0,)))
    shape = (experts, capacity, width)
    mixed_part = dot(weigh, partial_out.reshape(shape), over_slots).astype(BF16)
    grad_part = dot(pick, partial_back.reshape(shape), over_slots).astype(BF16)
    row_gate = jnp.sum(dy.astype(F32) * partial_out.astype(F32), axis=1).reshape(experts, capacity)
    gate_part = jnp.sum(pick.astype(F32) * row_gate[:, :, None], axis=1)
    gate_part = jnp.broadcast_to(gate_part[:, None, :], (experts, 8, local_tokens))
    mixed, grad_total, gate_all = reduce_all(pipes, experts, mixed_part, grad_part, gate_part)
    named = routes[:, :, None] == jnp.arange(experts)[None, None, :]
    grad_gates = jnp.sum(jnp.where(named, gate_all[:, 0, :].T[:, None, :], 0.0), axis=2)
    return (mixed, grad_total, grad_gates, grad_gate_w[None], grad_up_w[None], grad_down_w[None])


def solution(mesh):
    rows = P("expert", None)
    weights = P("expert", "pipe", None)
    return jax.shard_map(
        body,
        mesh=mesh,
        in_specs=(rows,) * 5 + (weights,) * 3,
        out_specs=(P("expert", "pipe"), P("expert", "pipe"), rows) + (weights,) * 3,
        check_vma=False,
    )
```
